128 devices in a mesh: gx: 8 (over x, core), yz: 16 (over z, y).
Axes of the slice: x: 4, y: 4, z: 4, core: 2. Of those that a mesh axis runs over, the one named last changes fastest.
Arguments:
- displacement: float32 [3, 64, 256, 2048], P(None, 'gx', 'yz'), may hold values from -1.2 to 1.2
- force: float32 [3, 64, 256, 2048], P(None, 'gx', 'yz'), may hold values from -1.2 to 1.2
- damage: float32 [64, 256, 2048], P('gx', 'yz'), may hold values from 0 to 0.6
- history_old: float32 [64, 256, 2048], P('gx', 'yz'), may hold values from 0 to 0.5
- material: int32 [64, 256, 2048], P('gx', 'yz'), may hold values from 0 to 3
- patch_ids: int32 [128, 12], P(('gx', 'yz')), may hold values from 0 to 15, as said below
- owners: int32 [128, 12, 1], P(('gx', 'yz')), may hold values from 0 to 15; in each aligned block of 12 rows (0 to 11, 12 to 23, ..., all dimensions but the last counted through in order) at most 2 rows name the same one
- toughness: float32 [128, 16, 2, 8, 16, 128], P(('gx', 'yz')), may hold values from 0.5 to 2
Outputs:
- new_displacement: float32 [3, 64, 256, 2048], P(None, 'gx', 'yz')
- history: float32 [64, 256, 2048], P('gx', 'yz')
- new_damage: float32 [64, 256, 2048], P('gx', 'yz')
The draws below stay inside these ranges and needn't reach their ends.
Inputs may be any that keep to these rules, and one draw needn't show every extreme that they name: `owners`: the entries of one device name one owner at most 2 times, and exactly 2 times in some devices. `patch_ids`: the 12 entries of one device are distinct.
All inputs are finite; a program needn't handle non-finite values.
Results may differ from the reference program's by a relative error of at most 0.0001.
Values sent between devices are 32-bit elements; how exact they have to be, the bound alone decides.
A program may use at most 128 MiB of HBM per device.

```python
import math
import jax
import jax.numpy as jnp
import numpy as np

CX = 8
CY = 16
CZ = 2048
PZ = 128
PL = 12
CAP = 2
MSTEPS = 2
SWEEPS = 8
PB = 16
NX = 64
NY = 256
N_GX = 8
N_YZ = 16
DEVICES = 128


def draw_patch_ids(key, part):
    keys = jax.random.split(key, DEVICES)
    orders = jax.vmap(lambda single: jax.random.permutation(single, CZ // PZ))(keys)
    return orders[:, :PL].astype(jnp.int32)


def touch_ends(drawn, own_key, low, top_value):
    place = [jax.random.randint(jax.random.fold_in(own_key, axis), (), 0, length) for axis, length in enumerate(drawn.shape)]
    widest = drawn.shape.index(max(drawn.shape))
    beside = place[:widest] + [(place[widest] + 1) % drawn.shape[widest]] + place[widest + 1:]
    return drawn.at[tuple(place)].set(low).at[tuple(beside)].set(top_value)


def block_scale(stream_key, dims, cuts, smallest, high):
    gain, own = 1.0, jax.random.fold_in(stream_key, 6)
    for axis_at, blocks in cuts:
        steps = jnp.exp(jax.random.uniform(jax.random.fold_in(own, axis_at), (blocks,), jnp.float32, smallest / len(cuts), high / len(cuts)))
        gain = gain * jnp.repeat(steps, dims[axis_at] // blocks).reshape([-1 if axis == axis_at else 1 for axis in range(len(dims))])
    return gain


def assign_block(stream_key, own, number, rows, count, top, most, lean):
    order = jax.random.permutation(stream_key, count)
    packed, ordinary = load_shares(count, rows * top, most, lean, True), load_shares(count, rows * top, most, lean, False)
    places = jnp.arange(count)

    def named(tallies, rotation):
        used = int((tallies > 0).sum())
        fixed = max(1, used // 4)
        passed = fixed + (places - fixed + rotation * (used - fixed)) % max(1, count - fixed)
        return jnp.zeros((count,), jnp.int32).at[order[jnp.where(places < fixed, places, passed)]].set(jnp.asarray(tallies, jnp.int32))

    tallies = jnp.where(number % 4 == 0, named(packed, number // 4), named(ordinary, number - number // 4 - 1))
    mixed = jax.random.permutation(jax.random.fold_in(own, 3), count)
    donor, receiver = mixed[0:count // 2 * 2:2], mixed[1:count // 2 * 2:2]
    slack = jnp.minimum(tallies[donor] - 1, most - tallies[receiver]) // 2
    slack = jnp.where((donor == order[0]) | (receiver == order[0]) | (tallies[receiver] == 0), 0, jnp.maximum(slack, 0))
    passed = jax.random.randint(jax.random.fold_in(own, 4), (count // 2,), 0, 1 << 20) % (slack + 1)
    tallies = tallies.at[donor].add(-passed).at[receiver].add(passed)
    labels = jnp.searchsorted(jnp.cumsum(tallies), jnp.arange(rows * top), side="right").astype(jnp.int32)
    grid = labels.reshape(top, rows).T
    grid = grid[jax.random.permutation(jax.random.fold_in(own, 1), rows)]
    rotation = jax.random.randint(jax.random.fold_in(own, 2), (rows, 1), 0, top)
    return jnp.take_along_axis(grid, (jnp.arange(top)[None, :] + rotation) % top, axis=1)


def load_shares(number_of, total, bound, skew, full):
    weights = [(1 << 20) // math.isqrt(standing ** skew) + 1 for standing in range(1, number_of + 1)]
    largest = bound if full else min(bound, max(-(-total // number_of), total * weights[0] // sum(weights)))
    least = 1 if total - largest >= number_of - 1 else 0
    counts, spare = [largest] + [least] * (number_of - 1), total - largest - least * (number_of - 1)
    while spare > 0:
        free = [i for i in range(1, number_of) if counts[i] < largest] or [i for i in range(1, number_of) if counts[i] < bound]
        pool, left = sum([weights[i] for i in free]), spare
        for i in free:
            addition = min(bound - counts[i], max(1, left * weights[i] // pool), spare)
            counts[i] = counts[i] + addition
            spare = spare - addition
    return np.array(counts)


def noise(rng, extent, scale, limit, pieces=(), held_as=jnp.bfloat16):
    loudness = block_scale(rng, extent, pieces, -0.22, 0.18) if pieces else 1.0
    array = jax.random.normal(rng, extent, jnp.float32) * scale * loudness
    return jnp.minimum(jnp.maximum(array, -limit), limit).astype(held_as)


def setup_inputs(seed: int = 0) -> dict:
    arg_keys = jax.random.split(jax.random.key(seed), 9)
    displacement = noise(arg_keys[0], (3, NX, NY, CZ), 0.2, 1.2, ((1, 8), (2, 16)), jnp.float32)
    force = noise(arg_keys[1], (3, NX, NY, CZ), 0.2, 1.2, ((1, 8), (2, 16)), jnp.float32)
    damage = jnp.clip(0.6 * jax.random.uniform(arg_keys[2], (NX, NY, CZ), jnp.float32) ** block_scale(arg_keys[2], (NX, NY, CZ), ((0, 8), (1, 16)), -0.2, 0.2), 0.0, 0.6)
    history_old = jnp.clip(0.5 * jax.random.uniform(arg_keys[3], (NX, NY, CZ), jnp.float32) ** block_scale(arg_keys[3], (NX, NY, CZ), ((0, 8), (1, 16)), -0.2, 0.2), 0.0, 0.5)
    material = touch_ends(jax.random.randint(arg_keys[4], (NX, NY, CZ), 0, 4), jax.random.fold_in(arg_keys[4], 1), 0, 3).astype(jnp.int32)
    patch_ids = draw_patch_ids(jax.random.fold_in(arg_keys[8], 71), 0)
    owners_keys = jax.random.split(jax.random.fold_in(arg_keys[6], 1), DEVICES * PL // PL)
    owners_turns = jax.random.permutation(jax.random.fold_in(arg_keys[6], 3), DEVICES * PL // PL)
    owners = jax.vmap(lambda own, number: assign_block(jax.random.fold_in(arg_keys[6], 2), own, number, PL, N_YZ, 1, CAP, 2))(owners_keys, owners_turns).reshape((DEVICES, PL, 1))
    toughness = jnp.clip(jnp.exp(math.log(2.0) - 1.3862944 * jax.random.uniform(arg_keys[7], (DEVICES, N_YZ, CAP, CX, CY, PZ), jnp.float32) ** block_scale(arg_keys[7], (DEVICES, N_YZ, CAP, CX, CY, PZ), ((0, 128),), -0.2, 0.2)), 0.5, 2.0)
    return dict(displacement=displacement, force=force, damage=damage, history_old=history_old, material=material, patch_ids=patch_ids, owners=owners, toughness=toughness)


MODULI = (1.0, 0.5, 4.0, 0.25)
SPRING = 0.05
RELAX = 0.8
LENGTH = 2.0


def modulus(material):
    result = jnp.zeros(material.shape, jnp.float32)
    for index, value in enumerate(MODULI):
        result = result + jnp.where(material == index, jnp.float32(value), jnp.float32(0.0))
    return result


def adjacent(padded):
    return [padded[..., 2:, 1:-1, 1:-1], padded[..., :-2, 1:-1, 1:-1],
            padded[..., 1:-1, 2:, 1:-1], padded[..., 1:-1, :-2, 1:-1],
            padded[..., 1:-1, 1:-1, 2:], padded[..., 1:-1, 1:-1, :-2]]


def zero_pad(field):
    widths = [(0, 0)] * (field.ndim - 3) + [(1, 1)] * 3
    return jnp.pad(field, widths)


def sweep(hist, start, tough):
    first = tough / LENGTH + 2.0 * hist
    second = tough * LENGTH
    denom = first + 6.0 * second
    value = start
    widths = [(0, 0)] * (value.ndim - 3) + [(1, 1)] * 3
    for step in range(SWEEPS):
        padded = jnp.pad(value, widths, mode="edge")
        total = sum(adjacent(padded))
        value = (2.0 * hist + second * total) / denom
    return jnp.maximum(value, start)


def to_patches(field):
    parts = field.reshape(N_GX, CX, N_YZ, CY, PB, PZ).transpose(0, 2, 4, 1, 3, 5)
    return parts.reshape(N_GX * N_YZ, PB, CX, CY, PZ)


def from_patches(parts):
    parts = parts.reshape(N_GX, N_YZ, PB, CX, CY, PZ).transpose(0, 3, 1, 4, 2, 5)
    return parts.reshape(N_GX * CX, N_YZ * CY, PB * PZ)


def reference(displacement, force, damage, history_old, material, patch_ids, owners, toughness):
    moduli = modulus(material)
    stiffness = moduli * ((1.0 - damage) ** 2 + 0.001)
    weights = [0.5 * (stiffness + other) for other in adjacent(zero_pad(stiffness))]
    diag = SPRING * stiffness + sum(weights)
    field = displacement
    for step in range(MSTEPS):
        near = adjacent(zero_pad(field))
        applied = SPRING * stiffness * field
        for weight, other in zip(weights, near):
            applied = applied + weight * (field - other)
        field = field + RELAX * (force - applied) / diag
    near = adjacent(zero_pad(field))
    squares = (near[0] - field) ** 2 + (near[2] - field) ** 2 + (near[4] - field) ** 2
    energy = 0.5 * moduli * jnp.sum(squares, axis=0)
    history = jnp.maximum(history_old, energy)
    owner_of = owners[:, :, 0]
    earlier = jnp.arange(PL)[None, :] < jnp.arange(PL)[:, None]
    same = owner_of[:, :, None] == owner_of[:, None, :]
    slot_rank = jnp.sum(jnp.where(same & earlier[None], 1, 0), axis=2).astype(jnp.int32)
    devices = jnp.arange(N_GX * N_YZ).astype(jnp.int32)
    source_yz = devices % N_YZ
    owner_dev = (devices // N_YZ)[:, None] * N_YZ + owner_of
    tough = toughness[owner_dev, source_yz[:, None], slot_rank]
    hist_parts = to_patches(history)[devices[:, None], patch_ids]
    damage_all = to_patches(damage)
    start = damage_all[devices[:, None], patch_ids]
    result = sweep(hist_parts, start, tough)
    damage_all = damage_all.at[devices[:, None], patch_ids].set(result)
    return field, history, from_patches(damage_all)
```

```python
import jax
import jax.numpy as jnp
from jax import lax
from jax.experimental import pallas as pl
from jax.experimental.pallas import tpu as pltpu
from jax.sharding import PartitionSpec as P

PZ = 128
PL = 12
CAP = 2
SWEEPS = 8
SPRING = 0.05
RELAX = 0.8
LENGTH = 2.0

CX = 8
CY = 16
NZ = 16
N_GX = 8
N_YZ = 16
SIDE = 4
R0 = 8
MESH = pl.DeviceIdType.MESH
F32 = jnp.float32

MOVES = [(1, 0), (3, 0), (2, 0), (0, 1), (0, 3), (1, 1), (3, 3), (1, 3), (3, 1),
         (2, 1), (2, 3), (0, 2), (1, 2), (3, 2), (2, 2)]
GROUPS = (6, 10, 15)
LATE = 4
FIRST = len(MOVES) - LATE
BATCH = 4
STAGES = ((4, 0), (4, 2), (2, 3), (2, 4))


def modulus(material):
    return jnp.where(
        material == 0,
        F32(1.0),
        jnp.where(material == 1, F32(0.5), jnp.where(material == 2, F32(4.0), F32(0.25))),
    )


def lane_masks():
    lane = lax.broadcasted_iota(jnp.int32, (8, PZ), 1)
    return lane == 0, lane == PZ - 1


def mechanics(ids, own, disp, force, damage, hist_old, material, tough, u2, hist, dmg, res, order,
              u0, u1, stiff, fbuf, mat, coef, wback, wahead, recv, home, late, grid_mat, line_mat, dcur, acur, bcur, keys,
              ld_sem, s_send, s_recv, u_send, u_recv, t_send, t_recv):
    gx = lax.axis_index("gx")
    yz = lax.axis_index("yz")
    my_z = yz // SIDE
    my_y = yz % SIDE
    x_low = gx > 0
    x_high = gx < N_GX - 1
    y_low = yz > 0
    y_high = yz < N_YZ - 1
    peers = [
        ((gx + N_GX - 1) % N_GX, yz),
        ((gx + 1) % N_GX, yz),
        (gx, (yz + N_YZ - 1) % N_YZ),
        (gx, (yz + 1) % N_YZ),
    ]
    exists = [x_low, x_high, y_low, y_high]

    def load(src, dst, sem):
        return pltpu.make_async_copy(src, dst, sem)

    zeros = jnp.zeros((8, PZ), F32)

    def clear_x(plane):
        def one(k, _):
            for half in range(2):
                rows = pl.ds(R0 + 8 * half, 8)
                stiff[plane, k, rows, :] = zeros
                for c in range(3):
                    u0[c, plane, k, rows, :] = zeros
                    u1[c, plane, k, rows, :] = zeros
                    u2[c, plane, k, rows, :] = zeros
            return 0
        lax.fori_loop(1, NZ + 1, one, 0)

    def clear_y(row):
        def one(x, _):
            for k in range(1, NZ + 1):
                rows = pl.ds(row, 8)
                stiff[x, k, rows, :] = zeros
                for c in range(3):
                    u0[c, x, k, rows, :] = zeros
                    u1[c, x, k, rows, :] = zeros
                    u2[c, x, k, rows, :] = zeros
            return 0
        lax.fori_loop(1, CX + 1, one, 0)

    def clear_z(x, _):
        for k in (0, NZ + 1):
            for half in range(2):
                rows = pl.ds(R0 + 8 * half, 8)
                stiff[x, k, rows, :] = zeros
                for c in range(3):
                    u0[c, x, k, rows, :] = zeros
                    u1[c, x, k, rows, :] = zeros
                    u2[c, x, k, rows, :] = zeros
        return 0

    lax.fori_loop(1, CX + 1, clear_z, 0)
    pl.when(jnp.logical_not(x_low))(lambda: clear_x(0))
    pl.when(jnp.logical_not(x_high))(lambda: clear_x(CX + 1))
    pl.when(jnp.logical_not(y_low))(lambda: clear_y(0))
    pl.when(jnp.logical_not(y_high))(lambda: clear_y(R0 + CY))

    def zs(k):
        return pl.ds(pl.multiple_of(k * PZ, PZ), PZ)

    def start_first(k, _):
        load(damage.at[:, :, zs(k)], dmg.at[:, k], ld_sem.at[0]).start()
        load(material.at[:, :, zs(k)], mat.at[:, k], ld_sem.at[1]).start()
        return 0

    def start_second(k, _):
        load(disp.at[:, :, :, zs(k)], u0.at[:, pl.ds(1, CX), k + 1, pl.ds(R0, CY), :], ld_sem.at[2]).start()
        load(force.at[:, :, :, zs(k)], fbuf.at[:, :, k], ld_sem.at[3]).start()
        load(hist_old.at[:, :, zs(k)], hist.at[:, k], ld_sem.at[4]).start()
        return 0

    lax.fori_loop(0, NZ, start_first, 0)
    lax.fori_loop(0, NZ, start_second, 0)
    mine = load(tough.at[yz], home, ld_sem.at[5])
    mine.start()

    barrier = pltpu.get_barrier_semaphore()
    for d in range(1, N_YZ):
        pl.semaphore_signal(barrier, inc=1, device_id=(gx, (yz + d) % N_YZ), device_id_type=MESH)
    for peer in peers[:2]:
        pl.semaphore_signal(barrier, inc=1, device_id=peer, device_id_type=MESH)
    pl.semaphore_wait(barrier, N_YZ + 1)

    def remote(src, dst, send, recv_s, peer):
        return pltpu.make_async_remote_copy(
            src_ref=src, dst_ref=dst, send_sem=send, recv_sem=recv_s,
            device_id=peer, device_id_type=MESH)

    for d in range(4):
        @pl.when(exists[d])
        def _(d=d):
            def one(k, _):
                if d == 0:
                    src, dst = disp.at[:, 0, :, zs(k)], u0.at[:, CX + 1, k + 1, pl.ds(R0, CY), :]
                elif d == 1:
                    src, dst = disp.at[:, CX - 1, :, zs(k)], u0.at[:, 0, k + 1, pl.ds(R0, CY), :]
                elif d == 2:
                    src = disp.at[:, :, pl.ds(0, 1), zs(k)]
                    dst = u0.at[:, pl.ds(1, CX), k + 1, pl.ds(R0 + CY, 1), :]
                else:
                    src = disp.at[:, :, pl.ds(CY - 1, 1), zs(k)]
                    dst = u0.at[:, pl.ds(1, CX), k + 1, pl.ds(R0 - 1, 1), :]
                remote(src, dst, u_send.at[0, d], u_recv.at[0, d], peers[d]).start()
                return 0
            lax.fori_loop(0, NZ, one, 0)

    ZIN = pl.ds(1, NZ)

    def s_copy(d, x):
        if d == 0:
            src, dst = stiff.at[1, ZIN, pl.ds(R0, CY), :], stiff.at[CX + 1, ZIN, pl.ds(R0, CY), :]
        elif d == 1:
            src, dst = stiff.at[CX, ZIN, pl.ds(R0, CY), :], stiff.at[0, ZIN, pl.ds(R0, CY), :]
        elif d == 2:
            src, dst = stiff.at[x, ZIN, pl.ds(R0, 1), :], stiff.at[x, ZIN, pl.ds(R0 + CY, 1), :]
        else:
            src, dst = stiff.at[x, ZIN, pl.ds(R0 + CY - 1, 1), :], stiff.at[x, ZIN, pl.ds(R0 - 1, 1), :]
        return remote(src, dst, s_send.at[d], s_recv.at[d], peers[d])

    def u_copy(buf, r, d, x):
        if d == 0:
            src, dst = buf.at[:, 1, ZIN, pl.ds(R0, CY), :], buf.at[:, CX + 1, ZIN, pl.ds(R0, CY), :]
        elif d == 1:
            src, dst = buf.at[:, CX, ZIN, pl.ds(R0, CY), :], buf.at[:, 0, ZIN, pl.ds(R0, CY), :]
        elif d == 2:
            src, dst = buf.at[:, x, ZIN, pl.ds(R0, 1), :], buf.at[:, x, ZIN, pl.ds(R0 + CY, 1), :]
        else:
            src, dst = buf.at[:, x, ZIN, pl.ds(R0 + CY - 1, 1), :], buf.at[:, x, ZIN, pl.ds(R0 - 1, 1), :]
        return remote(src, dst, u_send.at[r, d], u_recv.at[r, d], peers[d])

    every = pl.ds(1, CX)

    def send_planes(i, x, copy, dirs):
        for d in dirs:
            if d == 0:
                cond = jnp.logical_and(exists[d], i == 0)
            elif d == 1:
                cond = jnp.logical_and(exists[d], i == 1)
            else:
                cond = exists[d]
            pl.when(cond)(lambda d=d: copy(d, x).start())

    def wait_recvs(copy, dirs):
        for d in dirs:
            pl.when(exists[d ^ 1])(lambda d=d: copy(d, every).wait_recv())

    def wait_sends(copy, dirs):
        for d in dirs:
            pl.when(exists[d])(lambda d=d: copy(d, every).wait_send())

    def t_copy(m):
        dz, dy = MOVES[m]
        dst = (my_z + dz) % SIDE * SIDE + (my_y + dy) % SIDE
        slots = recv.at[yz] if m < FIRST else late[m - FIRST]
        return remote(tough.at[dst], slots, t_send.at[m], t_recv.at[m], (gx, dst))

    def plane_of(i):
        return 1 + (7 * i) % CX

    low_edge, high_edge = lane_masks()
    stencils(grid_mat, line_mat)

    def bytes_wait(src, dst, sem):
        load(src, dst, sem).wait()

    bytes_wait(dmg, dmg, ld_sem.at[0])
    bytes_wait(mat, mat, ld_sem.at[1])

    def stiff_plane(i, _):
        x = plane_of(i)
        for half in range(2):
            for k in range(NZ):
                part = (x - 1, k, pl.ds(8 * half, 8), slice(None))
                mod = modulus(mat[part])
                gap = 1.0 - dmg[part]
                stiff[x, k + 1, pl.ds(R0 + 8 * half, 8), :] = (0.5 * mod) * (gap * gap + 0.001)
        send_planes(i, x, s_copy, (0, 1, 2, 3))
        return 0

    lax.fori_loop(0, CX, stiff_plane, 0)

    def shifted(load_tile, k, mid):
        before = pltpu.roll(jnp.where(high_edge, load_tile(k - 1), mid), 1, 1)
        after = pltpu.roll(jnp.where(low_edge, load_tile(k + 1), mid), PZ - 1, 1)
        return before, after

    def z_faces(x, _):
        for half in range(2):
            here = pl.ds(R0 + 8 * half, 8)
            for k in range(1, NZ + 1):
                s = stiff[x, k, here, :]
                before, after = shifted(lambda kk: stiff[x, kk, here, :], k, s)
                part = (x - 1, k - 1, pl.ds(8 * half, 8), slice(None))
                wback[part] = s + before
                wahead[part] = s + after
        return 0


    for m in range(0, GROUPS[0]):
        t_copy(m).start()
    lax.fori_loop(1, CX + 1, z_faces, 0)

    bytes_wait(fbuf, fbuf, ld_sem.at[2])
    bytes_wait(fbuf, fbuf, ld_sem.at[3])
    bytes_wait(hist, hist, ld_sem.at[4])

    def u0_wait(d):
        return u_copy(u0, 0, d, every)

    wait_recvs(s_copy, (0, 1, 2, 3))
    wait_recvs(lambda d, x: u_copy(u0, 0, d, x), (0, 1, 2, 3))

    def relax(old, new, first, r, dirs):
        def plane(i, _):
            x = plane_of(i)
            for half in range(2):
                row = R0 + 8 * half
                here, back, ahead = pl.ds(row, 8), pl.ds(row - 1, 8), pl.ds(row + 1, 8)
                for k in range(1, NZ + 1):
                    part = (x - 1, k - 1, pl.ds(8 * half, 8), slice(None))
                    s = stiff[x, k, here, :]
                    w = [
                        s + stiff[x - 1, k, here, :],
                        s + stiff[x + 1, k, here, :],
                        s + stiff[x, k, back, :],
                        s + stiff[x, k, ahead, :],
                        wback[part],
                        wahead[part],
                    ]
                    if first:
                        total = (w[0] + w[1]) + (w[2] + w[3]) + (w[4] + w[5])
                        scale = RELAX / ((2.0 * SPRING) * s + total)
                        coef[part] = scale
                    else:
                        scale = coef[part]
                    for c in range(3):
                        u = old[c, x, k, here, :]
                        before, after = shifted(lambda kk: old[c, x, kk, here, :], k, u)
                        acc = w[0] * old[c, x - 1, k, here, :] + w[1] * old[c, x + 1, k, here, :]
                        acc = acc + (w[2] * old[c, x, k, back, :] + w[3] * old[c, x, k, ahead, :])
                        acc = acc + (w[4] * before + w[5] * after)
                        drive = fbuf[(c,) + part] + acc
                        new[c, x, k, here, :] = (1.0 - RELAX) * u + scale * drive
            send_planes(i, x, lambda d, xx: u_copy(new, r, d, xx), dirs)
            return 0
        lax.fori_loop(0, CX, plane, 0)

    relax(u0, u1, True, 1, (0, 1, 2, 3))
    for m in range(GROUPS[0], GROUPS[1]):
        t_copy(m).start()
    wait_recvs(lambda d, x: u_copy(u1, 1, d, x), (0, 1, 2, 3))

    relax(u1, u2, False, 2, (0, 2))
    for m in range(GROUPS[1], GROUPS[2]):
        t_copy(m).start()

    wait_recvs(lambda d, x: u_copy(u2, 2, d, x), (0, 2))

    def energy_plane(i, _):
        x = i + 1
        for half in range(2):
            row = R0 + 8 * half
            here, ahead = pl.ds(row, 8), pl.ds(row + 1, 8)
            for k in range(1, NZ + 1):
                part = (i, k - 1, pl.ds(8 * half, 8), slice(None))
                total = None
                for c in range(3):
                    u = u2[c, x, k, here, :]
                    after = jnp.where(low_edge, u2[c, x, k + 1, here, :], u)
                    a = u2[c, x + 1, k, here, :] - u
                    b = u2[c, x, k, ahead, :] - u
                    g = pltpu.roll(after, PZ - 1, 1) - u
                    term = a * a + b * b + g * g
                    total = term if total is None else total + term
                energy = (0.5 * modulus(mat[part])) * total
                hist[part] = jnp.maximum(hist[part], energy)
        return 0

    lax.fori_loop(0, CX, energy_plane, 0)

    def fill_key(j, _):
        owner = own[0, j]
        back_z = (my_z - owner // SIDE + SIDE) % SIDE
        back_y = (my_y - owner % SIDE + SIDE) % SIDE
        key = 0
        for c in range(LATE):
            dz, dy = MOVES[FIRST + c]
            key = key + jnp.where(jnp.logical_and(back_z == dz, back_y == dy), c + 1, 0)
        keys[0, j] = key
        slot = lax.fori_loop(0, j, lambda i, n: n + jnp.where(own[0, i] == owner, 1, 0), 0)
        keys[1, j] = jnp.minimum(slot, CAP - 1)
        return 0

    lax.fori_loop(0, PL, fill_key, 0)

    def fill_place(j, _):
        key = keys[0, j]

        def count(i, n):
            other = keys[0, i]
            before = jnp.logical_or(other < key, jnp.logical_and(other == key, i < j))
            return n + jnp.where(before, 1, 0)
        keys[2, j] = lax.fori_loop(0, PL, count, 0)
        return 0

    lax.fori_loop(0, PL, fill_place, 0)

    def fill_order(q, _):
        keys[3, q] = lax.fori_loop(0, PL, lambda i, n: n + jnp.where(keys[2, i] == q, i, 0), 0)
        return 0

    lax.fori_loop(0, PL, fill_order, 0)

    def fill_ids(q, _):
        order[0, q] = ids[0, keys[3, q]]
        return 0

    lax.fori_loop(0, PL, fill_ids, 0)

    mine.wait()
    cells = CX * CY

    def batch(first, size, arrived):
        def setup(b, _):
            q = first + b
            j = keys[3, q]
            key, slot, p = keys[0, j], keys[1, j], ids[0, j]
            g = jnp.where(own[0, j] == yz, home[slot], recv[own[0, j], slot])
            for c in range(arrived):
                g = jnp.where(key == c + 1, late[c][slot], g)
            g = g.reshape(cells, PZ)
            h2 = (2.0 * hist[:, p]).reshape(cells, PZ)
            g2 = g * LENGTH
            inv = 1.0 / (g / LENGTH + h2 + 6.0 * g2)
            acur[b] = h2 * inv
            bcur[b] = g2 * inv
            dcur[b] = dmg[:, p].reshape(cells, PZ)
            return 0

        lax.fori_loop(0, size, setup, 0)
        for b in range(size):
            res[first + b] = dcur[b].reshape(CX, CY, PZ)

        def sweep(step, _):
            line = line_mat[...]
            d = dcur[pl.ds(0, size)].reshape(size * cells, PZ)
            hi = d.astype(jnp.bfloat16)
            lo = (d - hi.astype(F32)).astype(jnp.bfloat16)
            zs_ = jnp.dot(jnp.concatenate([hi, lo], axis=1), line, preferred_element_type=F32)
            row = lax.broadcasted_iota(jnp.int32, (8, PZ), 0)
            first, last = row == 0, row == 7
            for b in range(size):
                news = []
                for x in range(CX):
                    base = CY * x
                    t0, t1 = dcur[b, pl.ds(base, 8), :], dcur[b, pl.ds(base + 8, 8), :]
                    lo0 = jnp.where(first, t0, pltpu.roll(t0, 1, 0))
                    hi1 = jnp.where(last, t1, pltpu.roll(t1, 7, 0))
                    y0 = lo0 + dcur[b, pl.ds(base + 1, 8), :]
                    y1 = dcur[b, pl.ds(base + 7, 8), :] + hi1
                    xm, xp = max(x - 1, 0) * CY, min(x + 1, CX - 1) * CY
                    for h, yy in ((0, y0), (1, y1)):
                        q = pl.ds(base + 8 * h, 8)
                        xs = dcur[b, pl.ds(xm + 8 * h, 8), :] + dcur[b, pl.ds(xp + 8 * h, 8), :]
                        r = b * cells + base + 8 * h
                        total = xs + yy + zs_[r:r + 8]
                        news.append((q, acur[b, q, :] + bcur[b, q, :] * total))
                for q, v in news:
                    dcur[b, q, :] = v
            return 0

        lax.fori_loop(0, SWEEPS, sweep, 0)
        for b in range(size):
            res[first + b] = jnp.maximum(dcur[b].reshape(CX, CY, PZ), res[first + b])

    for m in range(FIRST):
        t_copy(m).wait_recv()
    arrived = first = 0
    for size, needed in STAGES:
        for m in range(arrived, needed):
            t_copy(FIRST + m).wait_recv()
        arrived = needed
        batch(first, size, arrived)
        first += size

    wait_sends(s_copy, (0, 1, 2, 3))
    wait_sends(lambda d, x: u_copy(u0, 0, d, x), (0, 1, 2, 3))
    wait_sends(lambda d, x: u_copy(u1, 1, d, x), (0, 1, 2, 3))
    wait_sends(lambda d, x: u_copy(u2, 2, d, x), (0, 2))
    for m in range(len(MOVES)):
        t_copy(m).wait_send()


def stencils(grid_mat, line_mat):
    shape = (CX * CY, CX * CY)
    r = lax.broadcasted_iota(jnp.int32, shape, 0)
    c = lax.broadcasted_iota(jnp.int32, shape, 1)
    rx, ry = r // CY, r % CY
    cx, cy = c // CY, c % CY
    one, zero = F32(1.0), F32(0.0)

    def at(x, y):
        return jnp.where(jnp.logical_and(cx == x, cy == y), one, zero)

    grid = at(jnp.minimum(rx + 1, CX - 1), ry) + at(jnp.maximum(rx - 1, 0), ry)
    grid = grid + at(rx, jnp.minimum(ry + 1, CY - 1)) + at(rx, jnp.maximum(ry - 1, 0))
    grid = grid.astype(jnp.bfloat16)
    grid_mat[...] = jnp.concatenate([grid, grid], axis=1)
    shape = (PZ, PZ)
    r = lax.broadcasted_iota(jnp.int32, shape, 0)
    c = lax.broadcasted_iota(jnp.int32, shape, 1)
    line = jnp.where(r == jnp.minimum(c + 1, PZ - 1), one, zero) + jnp.where(r == jnp.maximum(c - 1, 0), one, zero)
    line = line.astype(jnp.bfloat16)
    line_mat[...] = jnp.concatenate([line, line], axis=0)


def write_out(order, u2, hist, dmg, res, u_out, hist_out, dmg_out, out_sem):
    def zs(k):
        return pl.ds(pl.multiple_of(k * PZ, PZ), PZ)

    def copy(src, dst, n):
        return pltpu.make_async_copy(src, dst, out_sem.at[n])

    def start(k, _):
        copy(u2.at[:, pl.ds(1, CX), k + 1, pl.ds(R0, CY), :], u_out.at[:, :, :, zs(k)], 0).start()
        copy(hist.at[:, k], hist_out.at[:, :, zs(k)], 1).start()
        return 0

    lax.fori_loop(0, NZ, start, 0)

    def start_damage(k, _):
        def find(q, found):
            hit = order[0, q] == k
            return jnp.where(hit, q + 1, found)

        found = lax.fori_loop(0, PL, find, 0)

        @pl.when(found == 0)
        def _():
            copy(dmg.at[:, k], dmg_out.at[:, :, zs(k)], 2).start()

        @pl.when(found > 0)
        def _():
            copy(res.at[found - 1], dmg_out.at[:, :, zs(k)], 2).start()
        return 0

    lax.fori_loop(0, NZ, start_damage, 0)
    whole = u2.at[:, pl.ds(1, CX), pl.ds(1, NZ), pl.ds(R0, CY), :]
    copy(whole, whole, 0).wait()
    copy(hist, hist, 1).wait()
    copy(dmg, dmg, 2).wait()


ANY = pl.BlockSpec(memory_space=pl.ANY)


def body(displacement, force, damage, history_old, material, patch_ids, owners, toughness):
    size = (CX, CY, NZ * PZ)
    padded = (3, CX + 2, NZ + 2, R0 + CY + 8, PZ)
    inner = (CX, NZ, CY, PZ)
    tough = toughness[0]
    patch = (CX, CY, PZ)
    slots = (CAP,) + patch
    smem = pl.BlockSpec(memory_space=pltpu.SMEM)
    vmem = pl.BlockSpec(memory_space=pltpu.VMEM)
    dma = pltpu.SemaphoreType.DMA
    field, history, old, solved, order = pl.pallas_call(
        mechanics,
        out_shape=(
            pltpu.VMEM(padded, F32),
            pltpu.VMEM(inner, F32),
            pltpu.VMEM(inner, F32),
            pltpu.VMEM((PL,) + patch, F32),
            jax.ShapeDtypeStruct((1, PL), jnp.int32),
        ),
        in_specs=[smem] * 2 + [ANY] * 6,
        out_specs=(vmem,) * 4 + (smem,),
        scratch_shapes=[
            pltpu.VMEM(padded, F32), pltpu.VMEM(padded, F32),
            pltpu.VMEM(padded[1:], F32),
            pltpu.VMEM((3,) + inner, F32),
            pltpu.VMEM(inner, jnp.int32), pltpu.VMEM(inner, F32),
            pltpu.VMEM(inner, F32), pltpu.VMEM(inner, F32),
            pltpu.VMEM((N_YZ,) + slots, F32),
            pltpu.VMEM(slots, F32),
            [pltpu.VMEM(slots, F32)] * LATE,
            pltpu.VMEM((CX * CY, 2 * CX * CY), jnp.bfloat16),
            pltpu.VMEM((2 * PZ, PZ), jnp.bfloat16),
            pltpu.VMEM((BATCH, CX * CY, PZ), F32),
            pltpu.VMEM((BATCH, CX * CY, PZ), F32),
            pltpu.VMEM((BATCH, CX * CY, PZ), F32),
            pltpu.SMEM((4, PL), jnp.int32),
            dma((6,)),
            dma((4,)), dma((4,)),
            dma((3, 4)), dma((3, 4)),
            dma((len(MOVES),)), dma((len(MOVES),)),
        ],
        compiler_params=pltpu.CompilerParams(
            collective_id=0, has_side_effects=True, vmem_limit_bytes=50 << 20),
    )(patch_ids, owners[:, :, 0], displacement, force, damage, history_old, material, tough)

    return pl.pallas_call(
        write_out,
        out_shape=(
            jax.ShapeDtypeStruct((3,) + size, F32),
            jax.ShapeDtypeStruct(size, F32),
            jax.ShapeDtypeStruct(size, F32),
        ),
        in_specs=[smem] + [vmem] * 4,
        out_specs=(ANY, ANY, ANY),
        scratch_shapes=[dma((3,))],
        compiler_params=pltpu.CompilerParams(vmem_limit_bytes=8 << 20),
    )(order, field, history, old, solved)


def solution(mesh):
    return jax.shard_map(
        body,
        mesh=mesh,
        in_specs=(
            P(None, "gx", "yz", None),
            P(None, "gx", "yz", None),
            P("gx", "yz", None),
            P("gx", "yz", None),
            P("gx", "yz", None),
            P(("gx", "yz"), None),
            P(("gx", "yz"), None, None),
            P(("gx", "yz"), None, None, None, None, None),
        ),
        out_specs=(P(None, "gx", "yz", None), P("gx", "yz", None), P("gx", "yz", None)),
        check_vma=False,
    )
```

```python
import jax
import jax.numpy as jnp
from jax import lax
from jax.experimental import pallas as pl
from jax.experimental.pallas import tpu as pltpu
from jax.sharding import PartitionSpec as P

PZ = 128
PL = 12
CAP = 2
SWEEPS = 8
SPRING = 0.05
RELAX = 0.8
LENGTH = 2.0

CX = 8
CY = 16
NZ = 16
N_GX = 8
N_YZ = 16
SIDE = 4
R0 = 8
MESH = pl.DeviceIdType.MESH
F32 = jnp.float32

MOVES = [(1, 0), (3, 0), (2, 0), (0, 1), (0, 3), (1, 1), (3, 3), (1, 3), (3, 1),
         (2, 1), (2, 3), (0, 2), (1, 2), (3, 2), (2, 2)]
GROUPS = (6, 10, 15)
LATE = 4
FIRST = len(MOVES) - LATE
BATCH = 4
STAGES = ((4, 0), (4, 2), (2, 3), (2, 4))


def modulus(material):
    return jnp.where(
        material == 0,
        F32(1.0),
        jnp.where(material == 1, F32(0.5), jnp.where(material == 2, F32(4.0), F32(0.25))),
    )


def lane_masks():
    lane = lax.broadcasted_iota(jnp.int32, (8, PZ), 1)
    return lane == 0, lane == PZ - 1


def mechanics(ids, own, disp, force, damage, hist_old, material, tough, u2, hist, fresh,
              dmg, res, spot, u0, u1, stiff, fbuf, mat, coef, wback, wahead, recv, home, late, grid_mat, line_mat, dcur, acur, bcur, keys,
              ld_sem, s_send, s_recv, u_send, u_recv, t_send, t_recv):
    gx = lax.axis_index("gx")
    yz = lax.axis_index("yz")
    my_z = yz // SIDE
    my_y = yz % SIDE
    x_low = gx > 0
    x_high = gx < N_GX - 1
    y_low = yz > 0
    y_high = yz < N_YZ - 1
    peers = [
        ((gx + N_GX - 1) % N_GX, yz),
        ((gx + 1) % N_GX, yz),
        (gx, (yz + N_YZ - 1) % N_YZ),
        (gx, (yz + 1) % N_YZ),
    ]
    exists = [x_low, x_high, y_low, y_high]

    def load(src, dst, sem):
        return pltpu.make_async_copy(src, dst, sem)

    zeros = jnp.zeros((8, PZ), F32)

    def clear_x(plane):
        def one(k, _):
            for half in range(2):
                rows = pl.ds(R0 + 8 * half, 8)
                stiff[plane, k, rows, :] = zeros
                for c in range(3):
                    u0[c, plane, k, rows, :] = zeros
                    u1[c, plane, k, rows, :] = zeros
                    u2[c, plane, k, rows, :] = zeros
            return 0
        lax.fori_loop(1, NZ + 1, one, 0)

    def clear_y(row):
        def one(x, _):
            for k in range(1, NZ + 1):
                rows = pl.ds(row, 8)
                stiff[x, k, rows, :] = zeros
                for c in range(3):
                    u0[c, x, k, rows, :] = zeros
                    u1[c, x, k, rows, :] = zeros
                    u2[c, x, k, rows, :] = zeros
            return 0
        lax.fori_loop(1, CX + 1, one, 0)

    def clear_z(x, _):
        for k in (0, NZ + 1):
            for half in range(2):
                rows = pl.ds(R0 + 8 * half, 8)
                stiff[x, k, rows, :] = zeros
                for c in range(3):
                    u0[c, x, k, rows, :] = zeros
                    u1[c, x, k, rows, :] = zeros
                    u2[c, x, k, rows, :] = zeros
        return 0

    lax.fori_loop(1, CX + 1, clear_z, 0)
    pl.when(jnp.logical_not(x_low))(lambda: clear_x(0))
    pl.when(jnp.logical_not(x_high))(lambda: clear_x(CX + 1))
    pl.when(jnp.logical_not(y_low))(lambda: clear_y(0))
    pl.when(jnp.logical_not(y_high))(lambda: clear_y(R0 + CY))

    def zs(k):
        return pl.ds(pl.multiple_of(k * PZ, PZ), PZ)

    def start_first(k, _):
        load(damage.at[:, :, zs(k)], dmg.at[:, k], ld_sem.at[0]).start()
        load(material.at[:, :, zs(k)], mat.at[:, k], ld_sem.at[1]).start()
        return 0

    def start_second(k, _):
        load(disp.at[:, :, :, zs(k)], u0.at[:, pl.ds(1, CX), k + 1, pl.ds(R0, CY), :], ld_sem.at[2]).start()
        load(force.at[:, :, :, zs(k)], fbuf.at[:, :, k], ld_sem.at[3]).start()
        load(hist_old.at[:, :, zs(k)], hist.at[:, k], ld_sem.at[4]).start()
        return 0

    lax.fori_loop(0, NZ, start_first, 0)
    lax.fori_loop(0, NZ, start_second, 0)
    mine = load(tough.at[yz], home, ld_sem.at[5])
    mine.start()

    barrier = pltpu.get_barrier_semaphore()
    for d in range(1, N_YZ):
        pl.semaphore_signal(barrier, inc=1, device_id=(gx, (yz + d) % N_YZ), device_id_type=MESH)
    for peer in peers[:2]:
        pl.semaphore_signal(barrier, inc=1, device_id=peer, device_id_type=MESH)
    pl.semaphore_wait(barrier, N_YZ + 1)

    def remote(src, dst, send, recv_s, peer):
        return pltpu.make_async_remote_copy(
            src_ref=src, dst_ref=dst, send_sem=send, recv_sem=recv_s,
            device_id=peer, device_id_type=MESH)

    for d in range(4):
        @pl.when(exists[d])
        def _(d=d):
            def one(k, _):
                if d == 0:
                    src, dst = disp.at[:, 0, :, zs(k)], u0.at[:, CX + 1, k + 1, pl.ds(R0, CY), :]
                elif d == 1:
                    src, dst = disp.at[:, CX - 1, :, zs(k)], u0.at[:, 0, k + 1, pl.ds(R0, CY), :]
                elif d == 2:
                    src = disp.at[:, :, pl.ds(0, 1), zs(k)]
                    dst = u0.at[:, pl.ds(1, CX), k + 1, pl.ds(R0 + CY, 1), :]
                else:
                    src = disp.at[:, :, pl.ds(CY - 1, 1), zs(k)]
                    dst = u0.at[:, pl.ds(1, CX), k + 1, pl.ds(R0 - 1, 1), :]
                remote(src, dst, u_send.at[0, d], u_recv.at[0, d], peers[d]).start()
                return 0
            lax.fori_loop(0, NZ, one, 0)

    ZIN = pl.ds(1, NZ)

    def s_copy(d, x):
        if d == 0:
            src, dst = stiff.at[1, ZIN, pl.ds(R0, CY), :], stiff.at[CX + 1, ZIN, pl.ds(R0, CY), :]
        elif d == 1:
            src, dst = stiff.at[CX, ZIN, pl.ds(R0, CY), :], stiff.at[0, ZIN, pl.ds(R0, CY), :]
        elif d == 2:
            src, dst = stiff.at[x, ZIN, pl.ds(R0, 1), :], stiff.at[x, ZIN, pl.ds(R0 + CY, 1), :]
        else:
            src, dst = stiff.at[x, ZIN, pl.ds(R0 + CY - 1, 1), :], stiff.at[x, ZIN, pl.ds(R0 - 1, 1), :]
        return remote(src, dst, s_send.at[d], s_recv.at[d], peers[d])

    def u_copy(buf, r, d, x):
        if d == 0:
            src, dst = buf.at[:, 1, ZIN, pl.ds(R0, CY), :], buf.at[:, CX + 1, ZIN, pl.ds(R0, CY), :]
        elif d == 1:
            src, dst = buf.at[:, CX, ZIN, pl.ds(R0, CY), :], buf.at[:, 0, ZIN, pl.ds(R0, CY), :]
        elif d == 2:
            src, dst = buf.at[:, x, ZIN, pl.ds(R0, 1), :], buf.at[:, x, ZIN, pl.ds(R0 + CY, 1), :]
        else:
            src, dst = buf.at[:, x, ZIN, pl.ds(R0 + CY - 1, 1), :], buf.at[:, x, ZIN, pl.ds(R0 - 1, 1), :]
        return remote(src, dst, u_send.at[r, d], u_recv.at[r, d], peers[d])

    every = pl.ds(1, CX)

    def send_planes(i, x, copy, dirs):
        for d in dirs:
            if d == 0:
                cond = jnp.logical_and(exists[d], i == 0)
            elif d == 1:
                cond = jnp.logical_and(exists[d], i == 1)
            else:
                cond = exists[d]
            pl.when(cond)(lambda d=d: copy(d, x).start())

    def wait_recvs(copy, dirs):
        for d in dirs:
            pl.when(exists[d ^ 1])(lambda d=d: copy(d, every).wait_recv())

    def wait_sends(copy, dirs):
        for d in dirs:
            pl.when(exists[d])(lambda d=d: copy(d, every).wait_send())

    def t_copy(m):
        dz, dy = MOVES[m]
        dst = (my_z + dz) % SIDE * SIDE + (my_y + dy) % SIDE
        slots = recv.at[yz] if m < FIRST else late[m - FIRST]
        return remote(tough.at[dst], slots, t_send.at[m], t_recv.at[m], (gx, dst))

    def plane_of(i):
        return 1 + (7 * i) % CX

    low_edge, high_edge = lane_masks()
    stencils(grid_mat, line_mat)

    def bytes_wait(src, dst, sem):
        load(src, dst, sem).wait()

    bytes_wait(dmg, dmg, ld_sem.at[0])
    bytes_wait(mat, mat, ld_sem.at[1])

    def stiff_plane(i, _):
        x = plane_of(i)
        for half in range(2):
            for k in range(NZ):
                part = (x - 1, k, pl.ds(8 * half, 8), slice(None))
                mod = modulus(mat[part])
                gap = 1.0 - dmg[part]
                stiff[x, k + 1, pl.ds(R0 + 8 * half, 8), :] = (0.5 * mod) * (gap * gap + 0.001)
        send_planes(i, x, s_copy, (0, 1, 2, 3))
        return 0

    lax.fori_loop(0, CX, stiff_plane, 0)

    def shifted(load_tile, k, mid):
        before = pltpu.roll(jnp.where(high_edge, load_tile(k - 1), mid), 1, 1)
        after = pltpu.roll(jnp.where(low_edge, load_tile(k + 1), mid), PZ - 1, 1)
        return before, after

    def z_faces(x, _):
        for half in range(2):
            here = pl.ds(R0 + 8 * half, 8)
            for k in range(1, NZ + 1):
                s = stiff[x, k, here, :]
                before, after = shifted(lambda kk: stiff[x, kk, here, :], k, s)
                part = (x - 1, k - 1, pl.ds(8 * half, 8), slice(None))
                wback[part] = s + before
                wahead[part] = s + after
        return 0


    for m in range(0, GROUPS[0]):
        t_copy(m).start()
    lax.fori_loop(1, CX + 1, z_faces, 0)

    bytes_wait(fbuf, fbuf, ld_sem.at[2])
    bytes_wait(fbuf, fbuf, ld_sem.at[3])
    bytes_wait(hist, hist, ld_sem.at[4])

    def u0_wait(d):
        return u_copy(u0, 0, d, every)

    wait_recvs(s_copy, (0, 1, 2, 3))
    wait_recvs(lambda d, x: u_copy(u0, 0, d, x), (0, 1, 2, 3))

    def relax(old, new, first, r, dirs):
        def plane(i, _):
            x = plane_of(i)
            for half in range(2):
                row = R0 + 8 * half
                here, back, ahead = pl.ds(row, 8), pl.ds(row - 1, 8), pl.ds(row + 1, 8)
                for k in range(1, NZ + 1):
                    part = (x - 1, k - 1, pl.ds(8 * half, 8), slice(None))
                    s = stiff[x, k, here, :]
                    w = [
                        s + stiff[x - 1, k, here, :],
                        s + stiff[x + 1, k, here, :],
                        s + stiff[x, k, back, :],
                        s + stiff[x, k, ahead, :],
                        wback[part],
                        wahead[part],
                    ]
                    if first:
                        total = (w[0] + w[1]) + (w[2] + w[3]) + (w[4] + w[5])
                        scale = RELAX / ((2.0 * SPRING) * s + total)
                        coef[part] = scale
                    else:
                        scale = coef[part]
                    for c in range(3):
                        u = old[c, x, k, here, :]
                        before, after = shifted(lambda kk: old[c, x, kk, here, :], k, u)
                        acc = w[0] * old[c, x - 1, k, here, :] + w[1] * old[c, x + 1, k, here, :]
                        acc = acc + (w[2] * old[c, x, k, back, :] + w[3] * old[c, x, k, ahead, :])
                        acc = acc + (w[4] * before + w[5] * after)
                        drive = fbuf[(c,) + part] + acc
                        new[c, x, k, here, :] = (1.0 - RELAX) * u + scale * drive
            send_planes(i, x, lambda d, xx: u_copy(new, r, d, xx), dirs)
            return 0
        lax.fori_loop(0, CX, plane, 0)

    relax(u0, u1, True, 1, (0, 1, 2, 3))
    for m in range(GROUPS[0], GROUPS[1]):
        t_copy(m).start()
    wait_recvs(lambda d, x: u_copy(u1, 1, d, x), (0, 1, 2, 3))

    relax(u1, u2, False, 2, (0, 2))
    for m in range(GROUPS[1], GROUPS[2]):
        t_copy(m).start()

    wait_recvs(lambda d, x: u_copy(u2, 2, d, x), (0, 2))

    def energy_plane(i, _):
        x = i + 1
        for half in range(2):
            row = R0 + 8 * half
            here, ahead = pl.ds(row, 8), pl.ds(row + 1, 8)
            for k in range(1, NZ + 1):
                part = (i, k - 1, pl.ds(8 * half, 8), slice(None))
                total = None
                for c in range(3):
                    u = u2[c, x, k, here, :]
                    after = jnp.where(low_edge, u2[c, x, k + 1, here, :], u)
                    a = u2[c, x + 1, k, here, :] - u
                    b = u2[c, x, k, ahead, :] - u
                    g = pltpu.roll(after, PZ - 1, 1) - u
                    term = a * a + b * b + g * g
                    total = term if total is None else total + term
                energy = (0.5 * modulus(mat[part])) * total
                hist[part] = jnp.maximum(hist[part], energy)
        return 0

    lax.fori_loop(0, CX, energy_plane, 0)

    def fill_key(j, _):
        owner = own[0, j]
        back_z = (my_z - owner // SIDE + SIDE) % SIDE
        back_y = (my_y - owner % SIDE + SIDE) % SIDE
        key = 0
        for c in range(LATE):
            dz, dy = MOVES[FIRST + c]
            key = key + jnp.where(jnp.logical_and(back_z == dz, back_y == dy), c + 1, 0)
        keys[0, j] = key
        slot = lax.fori_loop(0, j, lambda i, n: n + jnp.where(own[0, i] == owner, 1, 0), 0)
        keys[1, j] = jnp.minimum(slot, CAP - 1)
        return 0

    lax.fori_loop(0, PL, fill_key, 0)

    def fill_place(j, _):
        key = keys[0, j]

        def count(i, n):
            other = keys[0, i]
            before = jnp.logical_or(other < key, jnp.logical_and(other == key, i < j))
            return n + jnp.where(before, 1, 0)
        keys[2, j] = lax.fori_loop(0, PL, count, 0)
        return 0

    lax.fori_loop(0, PL, fill_place, 0)

    def fill_order(q, _):
        keys[3, q] = lax.fori_loop(0, PL, lambda i, n: n + jnp.where(keys[2, i] == q, i, 0), 0)
        return 0

    lax.fori_loop(0, PL, fill_order, 0)

    def fill_spot(k, _):
        def find(q, found):
            return jnp.where(ids[0, keys[3, q]] == k, q + 1, found)
        spot[k] = lax.fori_loop(0, PL, find, 0)
        return 0

    lax.fori_loop(0, NZ, fill_spot, 0)

    mine.wait()
    cells = CX * CY

    def batch(first, size, arrived):
        def setup(b, _):
            q = first + b
            j = keys[3, q]
            key, slot, p = keys[0, j], keys[1, j], ids[0, j]
            g = jnp.where(own[0, j] == yz, home[slot], recv[own[0, j], slot])
            for c in range(arrived):
                g = jnp.where(key == c + 1, late[c][slot], g)
            g = g.reshape(cells, PZ)
            h2 = (2.0 * hist[:, p]).reshape(cells, PZ)
            g2 = g * LENGTH
            inv = 1.0 / (g / LENGTH + h2 + 6.0 * g2)
            acur[b] = h2 * inv
            bcur[b] = g2 * inv
            dcur[b] = dmg[:, p].reshape(cells, PZ)
            return 0

        lax.fori_loop(0, size, setup, 0)
        for b in range(size):
            res[first + b] = dcur[b].reshape(CX, CY, PZ)

        def sweep(step, _):
            line = line_mat[...]
            d = dcur[pl.ds(0, size)].reshape(size * cells, PZ)
            hi = d.astype(jnp.bfloat16)
            lo = (d - hi.astype(F32)).astype(jnp.bfloat16)
            zs_ = jnp.dot(jnp.concatenate([hi, lo], axis=1), line, preferred_element_type=F32)
            row = lax.broadcasted_iota(jnp.int32, (8, PZ), 0)
            first, last = row == 0, row == 7
            for b in range(size):
                news = []
                for x in range(CX):
                    base = CY * x
                    t0, t1 = dcur[b, pl.ds(base, 8), :], dcur[b, pl.ds(base + 8, 8), :]
                    lo0 = jnp.where(first, t0, pltpu.roll(t0, 1, 0))
                    hi1 = jnp.where(last, t1, pltpu.roll(t1, 7, 0))
                    y0 = lo0 + dcur[b, pl.ds(base + 1, 8), :]
                    y1 = dcur[b, pl.ds(base + 7, 8), :] + hi1
                    xm, xp = max(x - 1, 0) * CY, min(x + 1, CX - 1) * CY
                    for h, yy in ((0, y0), (1, y1)):
                        q = pl.ds(base + 8 * h, 8)
                        xs = dcur[b, pl.ds(xm + 8 * h, 8), :] + dcur[b, pl.ds(xp + 8 * h, 8), :]
                        r = b * cells + base + 8 * h
                        total = xs + yy + zs_[r:r + 8]
                        news.append((q, acur[b, q, :] + bcur[b, q, :] * total))
                for q, v in news:
                    dcur[b, q, :] = v
            return 0

        lax.fori_loop(0, SWEEPS, sweep, 0)
        for b in range(size):
            res[first + b] = jnp.maximum(dcur[b].reshape(CX, CY, PZ), res[first + b])

    for m in range(FIRST):
        t_copy(m).wait_recv()
    arrived = first = 0
    for size, needed in STAGES:
        for m in range(arrived, needed):
            t_copy(FIRST + m).wait_recv()
        arrived = needed
        batch(first, size, arrived)
        first += size

    def settle(k, _):
        place = spot[k]
        fresh[k] = jnp.where(place > 0, res[jnp.maximum(place - 1, 0)], dmg[:, k])
        return 0

    lax.fori_loop(0, NZ, settle, 0)

    wait_sends(s_copy, (0, 1, 2, 3))
    wait_sends(lambda d, x: u_copy(u0, 0, d, x), (0, 1, 2, 3))
    wait_sends(lambda d, x: u_copy(u1, 1, d, x), (0, 1, 2, 3))
    wait_sends(lambda d, x: u_copy(u2, 2, d, x), (0, 2))
    for m in range(len(MOVES)):
        t_copy(m).wait_send()


def stencils(grid_mat, line_mat):
    shape = (CX * CY, CX * CY)
    r = lax.broadcasted_iota(jnp.int32, shape, 0)
    c = lax.broadcasted_iota(jnp.int32, shape, 1)
    rx, ry = r // CY, r % CY
    cx, cy = c // CY, c % CY
    one, zero = F32(1.0), F32(0.0)

    def at(x, y):
        return jnp.where(jnp.logical_and(cx == x, cy == y), one, zero)

    grid = at(jnp.minimum(rx + 1, CX - 1), ry) + at(jnp.maximum(rx - 1, 0), ry)
    grid = grid + at(rx, jnp.minimum(ry + 1, CY - 1)) + at(rx, jnp.maximum(ry - 1, 0))
    grid = grid.astype(jnp.bfloat16)
    grid_mat[...] = jnp.concatenate([grid, grid], axis=1)
    shape = (PZ, PZ)
    r = lax.broadcasted_iota(jnp.int32, shape, 0)
    c = lax.broadcasted_iota(jnp.int32, shape, 1)
    line = jnp.where(r == jnp.minimum(c + 1, PZ - 1), one, zero) + jnp.where(r == jnp.maximum(c - 1, 0), one, zero)
    line = line.astype(jnp.bfloat16)
    line_mat[...] = jnp.concatenate([line, line], axis=0)


def write_out(u2, hist, fresh, u_out, hist_out, dmg_out, out_sem):
    def zs(k):
        return pl.ds(pl.multiple_of(k * PZ, PZ), PZ)

    def copy(src, dst, n):
        return pltpu.make_async_copy(src, dst, out_sem.at[n])

    def start(k, _):
        copy(u2.at[:, pl.ds(1, CX), k + 1, pl.ds(R0, CY), :], u_out.at[:, :, :, zs(k)], 0).start()
        copy(hist.at[:, k], hist_out.at[:, :, zs(k)], 1).start()
        copy(fresh.at[k], dmg_out.at[:, :, zs(k)], 2).start()
        return 0

    lax.fori_loop(0, NZ, start, 0)
    whole = u2.at[:, pl.ds(1, CX), pl.ds(1, NZ), pl.ds(R0, CY), :]
    copy(whole, whole, 0).wait()
    copy(hist, hist, 1).wait()
    copy(fresh, fresh, 2).wait()


ANY = pl.BlockSpec(memory_space=pl.ANY)


def body(displacement, force, damage, history_old, material, patch_ids, owners, toughness):
    size = (CX, CY, NZ * PZ)
    padded = (3, CX + 2, NZ + 2, R0 + CY + 8, PZ)
    inner = (CX, NZ, CY, PZ)
    tough = toughness[0]
    patch = (CX, CY, PZ)
    slots = (CAP,) + patch
    smem = pl.BlockSpec(memory_space=pltpu.SMEM)
    vmem = pl.BlockSpec(memory_space=pltpu.VMEM)
    dma = pltpu.SemaphoreType.DMA
    field, history, fresh = pl.pallas_call(
        mechanics,
        out_shape=(
            pltpu.VMEM(padded, F32),
            pltpu.VMEM(inner, F32),
            pltpu.VMEM((NZ,) + patch, F32),
        ),
        in_specs=[smem] * 2 + [ANY] * 6,
        out_specs=(vmem,) * 3,
        scratch_shapes=[
            pltpu.VMEM(inner, F32), pltpu.VMEM((PL,) + patch, F32), pltpu.SMEM((NZ,), jnp.int32),
            pltpu.VMEM(padded, F32), pltpu.VMEM(padded, F32),
            pltpu.VMEM(padded[1:], F32),
            pltpu.VMEM((3,) + inner, F32),
            pltpu.VMEM(inner, jnp.int32), pltpu.VMEM(inner, F32),
            pltpu.VMEM(inner, F32), pltpu.VMEM(inner, F32),
            pltpu.VMEM((N_YZ,) + slots, F32),
            pltpu.VMEM(slots, F32),
            [pltpu.VMEM(slots, F32)] * LATE,
            pltpu.VMEM((CX * CY, 2 * CX * CY), jnp.bfloat16),
            pltpu.VMEM((2 * PZ, PZ), jnp.bfloat16),
            pltpu.VMEM((BATCH, CX * CY, PZ), F32),
            pltpu.VMEM((BATCH, CX * CY, PZ), F32),
            pltpu.VMEM((BATCH, CX * CY, PZ), F32),
            pltpu.SMEM((4, PL), jnp.int32),
            dma((6,)),
            dma((4,)), dma((4,)),
            dma((3, 4)), dma((3, 4)),
            dma((len(MOVES),)), dma((len(MOVES),)),
        ],
        compiler_params=pltpu.CompilerParams(
            collective_id=0, has_side_effects=True, vmem_limit_bytes=50 << 20),
    )(patch_ids, owners[:, :, 0], displacement, force, damage, history_old, material, tough)

    return pl.pallas_call(
        write_out,
        out_shape=(
            jax.ShapeDtypeStruct((3,) + size, F32),
            jax.ShapeDtypeStruct(size, F32),
            jax.ShapeDtypeStruct(size, F32),
        ),
        in_specs=[vmem] * 3,
        out_specs=(ANY, ANY, ANY),
        scratch_shapes=[dma((3,))],
        compiler_params=pltpu.CompilerParams(vmem_limit_bytes=8 << 20),
    )(field, history, fresh)


def solution(mesh):
    return jax.shard_map(
        body,
        mesh=mesh,
        in_specs=(
            P(None, "gx", "yz", None),
            P(None, "gx", "yz", None),
            P("gx", "yz", None),
            P("gx", "yz", None),
            P("gx", "yz", None),
            P(("gx", "yz"), None),
            P(("gx", "yz"), None, None),
            P(("gx", "yz"), None, None, None, None, None),
        ),
        out_specs=(P(None, "gx", "yz", None), P("gx", "yz", None), P("gx", "yz", None)),
        check_vma=False,
    )
```
